32 devices in a mesh: ctx: 8 (over z, y), head: 4 (over x, core).
Axes of the slice: x: 2, y: 2, z: 4, core: 2. Of those that a mesh axis runs over, the one named last changes fastest.
Arguments:
- signal: bfloat16 [4096, 4096], P('ctx', 'head'), may hold values from -6 to 6
- gate_input: bfloat16 [4096, 4096], P('ctx', 'head'), may hold values from -6 to 6
- input_map: bfloat16 [4096, 1024], P('ctx', 'head'), may hold values from -0.5 to 0.5
- readout: bfloat16 [4096, 1024], P('ctx', 'head'), may hold values from -0.5 to 0.5
- log_decay: float32 [64, 4096], P('head', 'ctx'), may hold values from -1.3 to 0
- skip_gain: float32 [64], P('head'), may hold values from 0.5 to 1.5
- norm_gain: float32 [4096], P('head'), may hold values from 0.5 to 1.5
- out_weight: bfloat16 [4096, 2048], P('head'), may hold values from -0.09375 to 0.09375
- out_grad: bfloat16 [4096, 2048], P(('ctx', 'head')), may hold values from -8 to 8
Outputs:
- layer_out: bfloat16 [4096, 2048], P(('ctx', 'head'))
- signal_grad: float32 [4096, 4096], P('ctx', 'head')
- gate_grad: float32 [4096, 4096], P('ctx', 'head')
- input_map_grad: float32 [4096, 1024], P('ctx', 'head')
- readout_grad: float32 [4096, 1024], P('ctx', 'head')
- decay_grad: float32 [64, 4096], P('head', 'ctx')
- skip_grad: float32 [64], P('head')
- gain_grad: float32 [4096], P('head')
- weight_grad: float32 [4096, 2048], P('head')
The draws below stay inside these ranges and needn't reach their ends.
All inputs are finite; a program needn't handle non-finite values.
Results may differ from the reference program's by a relative error of at most 0.0049.
Values may be sent and summed in bfloat16 or wider, within the bound.
A program may use at most 128 MiB of HBM per device.

```python
import math
from functools import partial
import jax
import jax.numpy as jnp
from jax import lax

D = 2048
HEADS = 64
P_SIZE = 64
N = 128
GROUPS = 8
SPAN = 256
TOKEN_TOTAL = 4096
INNER = 4096


def draw_log_decay(key, part):
    keys = jax.random.split(key, 7)
    slow_share = 0.5
    is_slow = jax.random.bernoulli(keys[0], slow_share, (HEADS, 1))
    slow_rate = jax.random.uniform(keys[1], (HEADS, 1), jnp.float32, 0.1, 0.5) / TOKEN_TOTAL
    fast_rate = jax.random.uniform(keys[2], (HEADS, 1), jnp.float32, 1.0 / 50.0, 1.0 / 30.0)
    reference_speed = jnp.where(is_slow, slow_rate, fast_rate)
    rough_multiplier = jax.random.uniform(keys[3], (HEADS, TOKEN_TOTAL), jnp.float32, 0.5, 1.5)
    block_log = jax.random.uniform(keys[4], (HEADS, TOKEN_TOTAL // SPAN), jnp.float32, math.log(0.5), math.log(2.0))
    tile_multiplier = jnp.repeat(jnp.exp(block_log), SPAN, axis=1)
    location_numbers = jax.random.randint(keys[5], (HEADS, 2, 1), 0, TOKEN_TOTAL)
    quantity_entries = jax.random.uniform(keys[6], (HEADS, 2, 1), jnp.float32, 0.2, 0.6)
    packet_clusters = jnp.sum(jnp.where(jnp.arange(TOKEN_TOTAL)[None, None, :] == location_numbers, quantity_entries, 0.0), axis=1)
    return -(reference_speed * rough_multiplier * tile_multiplier) - packet_clusters


def draw_out_grad(key, part):
    keys = jax.random.split(key, 1)
    ramp_up = 0.5 + 1.5 * jnp.arange(TOKEN_TOTAL, dtype=jnp.float32)[:, None] / TOKEN_TOTAL
    base_val = jax.random.normal(keys[0], (TOKEN_TOTAL, D), jnp.float32)
    return jnp.clip(base_val * ramp_up, -8.0, 8.0).astype(jnp.bfloat16)


def levels(stream_key, extent, shards, smallest, high):
    def one(dim, shards_of):
        draws = jax.random.uniform(jax.random.fold_in(jax.random.fold_in(stream_key, 6), dim), (shards_of,), jnp.float32, smallest / len(shards), high / len(shards))
        return jnp.repeat(jnp.exp(draws), extent[dim] // shards_of).reshape((-1,) + (1,) * (len(extent) - dim - 1))

    loudness = one(*shards[0])
    for cut in shards[1:]:
        loudness = loudness * one(*cut)
    return loudness


def noise(stream_key, shape, spread, bound, cuts=(), kind=jnp.bfloat16):
    drawn = spread * jax.random.normal(stream_key, shape, jnp.float32)
    if cuts:
        drawn = drawn * levels(stream_key, shape, cuts, -0.22, 0.18)
    return jnp.clip(drawn, -bound, bound).astype(kind)


def setup_inputs(seed: int = 0) -> dict:
    splits = jax.random.split(jax.random.key(seed), 10)
    return {
        "signal": noise(splits[0], (TOKEN_TOTAL, INNER), 1.0, 6.0, ((0, 8), (1, 4))),
        "gate_input": noise(splits[1], (TOKEN_TOTAL, INNER), 1.0, 6.0, ((0, 8), (1, 4))),
        "input_map": noise(splits[2], (TOKEN_TOTAL, GROUPS * N), N ** -0.5, 0.5, ((0, 8), (1, 4))),
        "readout": noise(splits[3], (TOKEN_TOTAL, GROUPS * N), N ** -0.5, 0.5, ((0, 8), (1, 4))),
        "log_decay": draw_log_decay(jax.random.fold_in(splits[9], 71), 0),
        "skip_gain": jnp.clip(0.5 + 1.0 * jax.random.uniform(splits[5], (HEADS,), jnp.float32) ** levels(splits[5], (HEADS,), ((0, 4),), -0.2, 0.2), 0.5, 1.5),
        "norm_gain": jnp.clip(0.5 + 1.0 * jax.random.uniform(splits[6], (INNER,), jnp.float32) ** levels(splits[6], (INNER,), ((0, 4),), -0.2, 0.2), 0.5, 1.5),
        "out_weight": noise(splits[7], (INNER, D), INNER ** -0.5, 0.09375, ((0, 4),)),
        "out_grad": draw_out_grad(jax.random.fold_in(splits[9], 71), 0),
    }


contract = partial(jnp.einsum, precision=lax.Precision.HIGHEST)

def span_parts(decay_log, map_f, read_f):
    cumulative = jnp.cumsum(decay_log, axis=-1)
    log_gap = cumulative[..., :, None] - cumulative[..., None, :]
    span_len = decay_log.shape[-1]
    lower_tri = jnp.arange(span_len)[:, None] >= jnp.arange(span_len)[None, :]
    lower_decay = jnp.where(lower_tri, jnp.exp(jnp.minimum(log_gap, 0.0)), 0.0)
    inner_prod = contract('ign,jgn->gij', read_f, map_f)
    mixing = lower_decay * inner_prod[:, None]
    to_closing = jnp.exp(cumulative[..., -1:] - cumulative)
    from_start = jnp.moveaxis(jnp.exp(cumulative), -1, 0)
    return (cumulative, lower_decay, mixing, to_closing, from_start)

def forward_step(carry_state, span_item):
    decay_log, signal_f, map_f, read_f = span_item
    cumulative, lower_decay, mixing, to_closing, from_start = span_parts(decay_log, map_f, read_f)
    core_out = contract('ghij,jghp->ighp', mixing, signal_f)
    core_out = core_out + from_start[..., None] * contract('ghpn,ign->ighp', carry_state, read_f)
    next_state = jnp.exp(cumulative[..., -1])[..., None, None] * carry_state
    next_state = next_state + contract('ghj,jghp,jgn->ghpn', to_closing, signal_f, map_f)
    return (next_state, (core_out, carry_state))

def backward_step(carry_grad, span_item):
    decay_log, signal_f, map_f, read_f, grad_y, core_out, carry_state = span_item
    cumulative, lower_decay, mixing, to_closing, from_start = span_parts(decay_log, map_f, read_f)
    core_grad = contract('ghij,ighp->jghp', mixing, grad_y)
    core_grad = core_grad + contract('ghj,ghpn,jgn->jghp', to_closing, carry_grad, map_f)
    pair_grad = contract('ighp,jghp->ghij', grad_y, signal_f) * lower_decay
    map_grad = contract('ghij,ign->jgn', pair_grad, read_f)
    map_grad = map_grad + contract('ghj,ghpn,jghp->jgn', to_closing, carry_grad, signal_f)
    read_grad = contract('ghij,jgn->ign', pair_grad, map_f)
    read_grad = read_grad + contract('igh,ghpn,ighp->ign', from_start, carry_state, grad_y)
    earlier_grad = jnp.exp(cumulative[..., -1])[..., None, None] * carry_grad
    earlier_grad = earlier_grad + contract('igh,ighp,ign->ghpn', from_start, grad_y, read_f)
    log_slope = lax.optimization_barrier(jnp.sum(grad_y * core_out - signal_f * core_grad, axis=-1))
    return (earlier_grad, (core_grad, map_grad, read_grad, log_slope))

def reference(signal, gate_input, input_map, readout, log_decay, skip_gain, norm_gain, out_weight, out_grad):
    length = signal.shape[0]
    span_count = length // SPAN
    heads_group = HEADS // GROUPS
    group_width = heads_group * P_SIZE
    signal_f = signal.astype(jnp.float32).reshape(span_count, SPAN, GROUPS, heads_group, P_SIZE)
    map_f = input_map.astype(jnp.float32).reshape(span_count, SPAN, GROUPS, N)
    read_f = readout.astype(jnp.float32).reshape(span_count, SPAN, GROUPS, N)
    decay_log = log_decay.reshape(GROUPS, heads_group, span_count, SPAN).transpose(2, 0, 1, 3)
    skip_scale = skip_gain.reshape(GROUPS, heads_group)[:, :, None]
    initial = jnp.zeros((GROUPS, heads_group, P_SIZE, N), jnp.float32)
    last_state, (core_out, entry_state) = lax.scan(forward_step, initial, (decay_log, signal_f, map_f, read_f))
    with_skip = (core_out + skip_scale * signal_f).reshape(length, GROUPS, group_width)
    gate_f = gate_input.astype(jnp.float32).reshape(length, GROUPS, group_width)
    sigmoid_gate = jax.nn.sigmoid(gate_f)
    silu_gate = gate_f * sigmoid_gate
    gated_out = with_skip * silu_gate
    inv_rms = lax.rsqrt(lax.optimization_barrier(jnp.mean(gated_out * gated_out, axis=-1, keepdims=True)) + 1e-05)
    gain_f = norm_gain.reshape(GROUPS, group_width)
    normed = (gated_out * inv_rms * gain_f).reshape(length, INNER).astype(jnp.bfloat16)
    layer_out = jnp.dot(normed, out_weight, preferred_element_type=jnp.float32).astype(jnp.bfloat16)
    dnormed = jnp.dot(out_grad, out_weight.T, preferred_element_type=jnp.float32).astype(jnp.bfloat16)
    dnormed = lax.optimization_barrier(dnormed).astype(jnp.float32).reshape(length, GROUPS, group_width)
    weight_grad = jnp.dot(normed.T, out_grad, preferred_element_type=jnp.float32)
    gain_grad = lax.optimization_barrier(jnp.sum(dnormed * gated_out * inv_rms, axis=0)).reshape(INNER)
    scaled_grad = gain_f * dnormed
    dgated = inv_rms * scaled_grad - gated_out * inv_rms ** 3 * lax.optimization_barrier(jnp.mean(scaled_grad * gated_out, axis=-1, keepdims=True))
    gate_grad = (dgated * with_skip * sigmoid_gate * (1.0 + gate_f * (1.0 - sigmoid_gate))).reshape(length, INNER)
    grad_y = (dgated * silu_gate).reshape(span_count, SPAN, GROUPS, heads_group, P_SIZE)
    skip_grad = lax.optimization_barrier(jnp.sum(grad_y * signal_f, axis=(0, 1, 4))).reshape(HEADS)
    first_grad, (core_grad, map_grad, read_grad, log_slope) = lax.scan(backward_step, jnp.zeros((GROUPS, heads_group, P_SIZE, N), jnp.float32), (decay_log, signal_f, map_f, read_f, grad_y, core_out, entry_state), reverse=True)
    signal_grad = (core_grad + skip_scale * grad_y).reshape(length, INNER)
    decay_grad = log_slope.transpose(2, 3, 0, 1).reshape(HEADS, length)
    return (layer_out, signal_grad, gate_grad, map_grad.reshape(length, GROUPS * N), read_grad.reshape(length, GROUPS * N), decay_grad, skip_grad, gain_grad, weight_grad)
```

```python
from functools import partial

import jax
import jax.numpy as jnp
from jax import lax
from jax.experimental import pallas as pl
from jax.experimental.pallas import tpu as pltpu
from jax.sharding import PartitionSpec as P

P_SIZE = 64
N = 128
CHUNK = 256
F32 = jnp.float32
BF16 = jnp.bfloat16
VMEM_LIMIT = 52 * 1024 * 1024

NN = (((1,), (0,)), ((), ()))
NT = (((1,), (1,)), ((), ()))
TN = (((0,), (0,)), ((), ()))


def mm(a, b, dims=NN):
    return lax.dot_general(a, b, dims, preferred_element_type=F32)


def spread(factor, width):
    rows = factor.shape[0]
    left = lax.broadcasted_iota(jnp.int32, (rows, 128), 1) < P_SIZE
    pairs = []
    for k in range(width // 128):
        a = jnp.broadcast_to(factor[:, 2 * k : 2 * k + 1], (rows, 128))
        b = jnp.broadcast_to(factor[:, 2 * k + 1 : 2 * k + 2], (rows, 128))
        pairs.append(jnp.where(left, a, b))
    return jnp.concatenate(pairs, axis=1)


def cumulated(log_row):
    heads, length = log_row.shape
    hi = log_row.astype(BF16).astype(F32)
    rest = log_row - hi
    mid = rest.astype(BF16).astype(F32)
    low = rest - mid
    parts = jnp.concatenate([hi, mid, low, jnp.zeros_like(hi)], axis=0).astype(BF16)
    upper = (
        lax.broadcasted_iota(jnp.int32, (length, length), 0)
        <= lax.broadcasted_iota(jnp.int32, (length, length), 1)
    )
    sums = mm(parts, jnp.where(upper, 1.0, 0.0).astype(BF16))
    row = sums[0:heads] + sums[heads : 2 * heads] + sums[2 * heads : 3 * heads]
    col = jnp.transpose(jnp.concatenate([row] * (128 // heads), axis=0))
    return row, col


def decays(col, width):
    heads = width // P_SIZE
    col = col[:, :heads]
    from_start = jnp.exp(col)
    to_closing = jnp.exp(col[-1:, :] - col)
    return spread(from_start, width), spread(to_closing, width)


def chunks_of(total):
    return [(c, slice(c * CHUNK, (c + 1) * CHUNK)) for c in range(total // CHUNK)]


def in_parts(values):
    width = values[0].shape[1]
    at = lax.broadcasted_iota(jnp.int32, (8, width), 0)
    rows = jnp.zeros((8, width), F32)
    for i, value in enumerate(values):
        hi = value.astype(BF16).astype(F32)
        mid = (value - hi).astype(BF16).astype(F32)
        for j, part in enumerate((hi, mid, value - hi - mid)):
            rows = jnp.where(at == 3 * i + j, part, rows)
    return rows.astype(BF16)


def local_state_kernel(x_ref, b_ref, log_ref, state_ref, decay_ref):
    tokens, width = x_ref.shape
    state = jnp.zeros((N, width), F32)
    decay = jnp.ones((1, width), F32)
    for _, at in chunks_of(tokens):
        _, col = cumulated(log_ref[:, at])
        from_start, to_closing = decays(col, width)
        span = from_start[-1:, :]
        scaled = (x_ref[at, :].astype(F32) * to_closing).astype(BF16)
        state = state * span + mm(b_ref[at, :], scaled, TN)
        decay = decay * span
    state_ref[0] = state.astype(BF16)
    decay_ref[0] = in_parts([decay])


def forward_kernel(
    x_ref, z_ref, b_ref, c_ref, log_ref, skip_ref, gain_ref, incoming_ref, rows_ref,
    core_ref, entry_ref, normed_ref, weight_ref,
):
    tokens, width = x_ref.shape
    state = incoming_ref[0].astype(F32)
    left = lax.broadcasted_iota(jnp.int32, (CHUNK, 128), 1) < P_SIZE
    lower = (
        lax.broadcasted_iota(jnp.int32, (CHUNK, CHUNK), 0)
        >= lax.broadcasted_iota(jnp.int32, (CHUNK, CHUNK), 1)
    )
    last = tokens // CHUNK - 1
    for c, at in chunks_of(tokens):
        row, col = cumulated(log_ref[:, at])
        from_start, to_closing = decays(col, width)
        x = x_ref[at, :]
        xf = x.astype(F32)
        bm, cm = b_ref[at, :], c_ref[at, :]
        inner = mm(cm, bm, NT)
        entry = state.astype(BF16)
        entry_ref[0, c] = entry
        pieces = []
        for k in range(width // 128):
            pair = x[:, 128 * k : 128 * k + 128]
            halves = []
            for h in (2 * k, 2 * k + 1):
                gap = jnp.where(lower, col[:, h : h + 1] - row[h : h + 1, :], -1e30)
                halves.append(mm((jnp.exp(gap) * inner).astype(BF16), pair))
            pieces.append(jnp.where(left, halves[0], halves[1]))
        core = jnp.concatenate(pieces, axis=1) + from_start * mm(cm, entry)
        core_ref[at, :] = core
        y = core + skip_ref[...] * xf
        z = z_ref[at, :].astype(F32)
        gated = y * (z * jax.nn.sigmoid(z))
        inv = lax.rsqrt(jnp.mean(gated * gated, axis=1, keepdims=True) + 1e-05)
        normed_ref[at, :] = (gated * inv * gain_ref[...]).astype(BF16)
        if c < last:
            scaled = (xf * to_closing).astype(BF16)
            state = state * from_start[-1:, :] + mm(bm, scaled, TN)
    columns = rows_ref.shape[1]
    tile = 512
    for n in range(columns // tile):
        cut = slice(n * tile, (n + 1) * tile)
        weight_ref[:, cut] = mm(normed_ref[...], rows_ref[:, cut], TN).astype(BF16)


def middle_kernel(
    x_ref, z_ref, c_ref, log_ref, skip_ref, gain_ref, core_ref, normed_ref, w_ref, rows_ref,
    layer_ref, dy_ref, gate_ref, later_ref, part_ref, total,
):
    tokens, width = x_ref.shape
    group = pl.program_id(0)
    groups = pl.num_programs(0)
    outflow = jnp.zeros((N, width), F32)
    gain_sum = jnp.zeros((1, width), F32)
    skip_sum = jnp.zeros((1, width), F32)
    gain = gain_ref[...]
    for _, at in reversed(chunks_of(tokens)):
        _, col = cumulated(log_ref[:, at])
        from_start = spread(jnp.exp(col[:, : width // P_SIZE]), width)
        dn = mm(rows_ref[at, :], w_ref[...], NT).astype(BF16).astype(F32)
        xf = x_ref[at, :].astype(F32)
        z = z_ref[at, :].astype(F32)
        y = core_ref[at, :] + skip_ref[...] * xf
        s = jax.nn.sigmoid(z)
        silu = z * s
        gated = y * silu
        inv = lax.rsqrt(jnp.mean(gated * gated, axis=1, keepdims=True) + 1e-05)
        gain_sum += jnp.sum(dn * gated * inv, axis=0, keepdims=True)
        scaled = gain * dn
        mean = jnp.mean(scaled * gated, axis=1, keepdims=True)
        dgated = inv * scaled - gated * (inv * inv * inv * mean)
        gate_ref[at, :] = dgated * y * s * (1.0 + z * (1.0 - s))
        dy = dgated * silu
        dy_ref[at, :] = dy
        skip_sum += jnp.sum(dy * xf, axis=0, keepdims=True)
        outflow = outflow * from_start[-1:, :] + mm(
            c_ref[at, :], (dy * from_start).astype(BF16), TN
        )
    later_ref[0] = outflow.astype(BF16)
    part_ref[0] = in_parts([gain_sum, skip_sum])
    columns = w_ref.shape[1]
    tile = 512
    for n in range(columns // tile):
        cut = slice(n * tile, (n + 1) * tile)
        piece = mm(normed_ref[...], w_ref[:, cut])

        @pl.when(group == 0)
        def _():
            total[:, cut] = piece

        @pl.when(group > 0)
        def _():
            total[:, cut] += piece

    @pl.when(group == groups - 1)
    def _():
        layer_ref[...] = total[...].astype(BF16)


def backward_kernel(
    x_ref, dy_ref, core_ref, b_ref, c_ref, log_ref, skip_ref, entry_ref, later_ref,
    signal_ref, map_ref, read_ref, decay_ref,
):
    tokens, width = x_ref.shape
    heads = width // P_SIZE
    outflow = later_ref[0].astype(F32)
    left = lax.broadcasted_iota(jnp.int32, (CHUNK, 128), 1) < P_SIZE
    upper = (
        lax.broadcasted_iota(jnp.int32, (CHUNK, CHUNK), 0)
        <= lax.broadcasted_iota(jnp.int32, (CHUNK, CHUNK), 1)
    )
    own = (
        lax.broadcasted_iota(jnp.int32, (heads, width), 1) // P_SIZE
        == lax.broadcasted_iota(jnp.int32, (heads, width), 0)
    )
    own = jnp.where(own, 1.0, 0.0).astype(BF16)
    for c, at in reversed(chunks_of(tokens)):
        row, col = cumulated(log_ref[:, at])
        from_start, to_closing = decays(col, width)
        x = x_ref[at, :]
        xf = x.astype(F32)
        dyf = dy_ref[at, :]
        dy = dyf.astype(BF16)
        bm, cm = b_ref[at, :], c_ref[at, :]
        inner = mm(bm, cm, NT)
        out = outflow.astype(BF16)
        pair_sum = jnp.zeros((CHUNK, CHUNK), F32)
        pieces = []
        for k in range(width // 128):
            cut = slice(128 * k, 128 * k + 128)
            x_pair, dy_pair = x[:, cut], dy[:, cut]
            halves = []
            for h, side in ((2 * k, left), (2 * k + 1, ~left)):
                gap = jnp.where(upper, row[h : h + 1, :] - col[:, h : h + 1], -1e30)
                fade = jnp.exp(gap)
                halves.append(mm((fade * inner).astype(BF16), dy_pair))
                one = jnp.where(side, xf[:, cut], 0.0).astype(BF16)
                pair_sum += mm(one, dy_pair, NT) * fade
            pieces.append(jnp.where(left, halves[0], halves[1]))
        core_grad = jnp.concatenate(pieces, axis=1) + to_closing * mm(bm, out)
        signal_ref[at, :] = core_grad + skip_ref[...] * dyf
        pair_sum = pair_sum.astype(BF16)
        map_ref[at, :] = mm(pair_sum, cm) + mm((xf * to_closing).astype(BF16), out, NT)
        dy_start = (dyf * from_start).astype(BF16)
        read_ref[at, :] = mm(pair_sum, bm, TN) + mm(dy_start, entry_ref[0, c], NT)
        slope = dyf * core_ref[at, :] - xf * core_grad
        hi = slope.astype(BF16)
        low = (slope - hi.astype(F32)).astype(BF16)
        decay_ref[:, at] = mm(own, hi, NT) + mm(own, low, NT)
        if c > 0:
            outflow = outflow * from_start[-1:, :] + mm(cm, dy_start, TN)


def params():
    return pltpu.CompilerParams(
        dimension_semantics=("arbitrary",), vmem_limit_bytes=VMEM_LIMIT
    )


def cost(flops, moved, exps=0):
    return pl.CostEstimate(flops=int(flops), bytes_accessed=int(moved), transcendentals=int(exps))


def entering(state, extra, reverse, fades=None):
    devices = lax.axis_size("ctx")
    groups, depth, width = state.shape
    share = depth // devices
    shares = state.reshape(groups, devices, share, width).transpose(1, 0, 2, 3)
    copies = jnp.broadcast_to(extra[None], (devices,) + extra.shape)
    sent = jnp.concatenate([shares, copies], axis=2)
    every = lax.all_to_all(sent, "ctx", split_axis=0, concat_axis=0, tiled=True)
    extras = every[:, :, share:].astype(F32)
    if fades is None:
        fades = jnp.sum(extras[:, :, 0:3], axis=2, keepdims=True)
    carried = jnp.zeros((groups, share, width), F32)
    found = [None] * devices
    for d in reversed(range(devices)) if reverse else range(devices):
        found[d] = carried.astype(BF16)
        carried = fades[d] * carried + every[d, :, :share].astype(F32)
    back = lax.all_to_all(jnp.stack(found), "ctx", split_axis=0, concat_axis=0, tiled=True)
    return back.transpose(1, 0, 2, 3).reshape(groups, depth, width), extras, fades


def summed(part, axis):
    devices = lax.axis_size(axis)
    rows, columns = part.shape
    terms = lax.all_to_all(part, axis, split_axis=0, concat_axis=0, tiled=True)
    terms = terms.reshape(devices, rows // devices, columns)
    return jnp.sum(terms.astype(F32), axis=0).astype(BF16)


def on_device(
    signal, gate_input, input_map, readout, log_decay, skip_gain, norm_gain, out_weight, out_grad
):
    tokens, features = signal.shape
    heads = log_decay.shape[0]
    groups = input_map.shape[1] // N
    in_group = heads // groups
    width = in_group * P_SIZE
    model = out_weight.shape[1]
    spans = tokens // CHUNK
    sds = jax.ShapeDtypeStruct
    wide = pl.BlockSpec((tokens, width), lambda g: (0, g))
    narrow = pl.BlockSpec((tokens, N), lambda g: (0, g))
    logs = pl.BlockSpec((in_group, tokens), lambda g: (g, 0))
    lane = pl.BlockSpec((1, width), lambda g: (0, g))
    state = pl.BlockSpec((1, N, width), lambda g: (g, 0, 0))
    fade = pl.BlockSpec((1, 8, width), lambda g: (g, 0, 0))
    entries = pl.BlockSpec((1, spans, N, width), lambda g: (g, 0, 0, 0))
    weight = pl.BlockSpec((width, model), lambda g: (g, 0))
    rows = pl.BlockSpec((tokens, model), lambda g: (0, 0))

    skip = jnp.repeat(skip_gain, P_SIZE).reshape(1, features)
    gain = norm_gain.reshape(1, features)
    piece = lax.all_gather(out_grad, "head", axis=0, tiled=True)

    own_state, own_fade = pl.pallas_call(
        local_state_kernel,
        grid=(groups,),
        in_specs=[wide, narrow, logs],
        out_specs=[state, fade],
        out_shape=[sds((groups, N, width), BF16), sds((groups, 8, width), BF16)],
        compiler_params=params(),
        cost_estimate=cost(2 * tokens * N * features, 3 * tokens * features),
        name="local_state",
    )(signal, input_map, log_decay)
    incoming, _, fades = entering(own_state, own_fade, False)

    core, entry, normed, weight_part = pl.pallas_call(
        forward_kernel,
        grid=(groups,),
        in_specs=[wide, wide, narrow, narrow, logs, lane, lane, state, rows],
        out_specs=[wide, entries, wide, weight],
        out_shape=[
            sds((tokens, features), F32),
            sds((groups, spans, N, width), BF16),
            sds((tokens, features), BF16),
            sds((features, model), BF16),
        ],
        compiler_params=params(),
        cost_estimate=cost(2 * tokens * features * model, 12 * tokens * features),
        name="forward",
    )(signal, gate_input, input_map, readout, log_decay, skip, gain, incoming, piece)
    weight_share = summed(weight_part, "ctx")
    weight_grad = lax.all_gather(weight_share, "ctx", axis=0, tiled=True).astype(F32)

    layer_part, dy, gate_grad, own_later, parts = pl.pallas_call(
        middle_kernel,
        grid=(groups,),
        in_specs=[wide, wide, narrow, logs, lane, lane, wide, wide, weight, rows],
        out_specs=[rows, wide, wide, state, fade],
        out_shape=[
            sds((tokens, model), BF16),
            sds((tokens, features), F32),
            sds((tokens, features), F32),
            sds((groups, N, width), BF16),
            sds((groups, 8, width), BF16),
        ],
        scratch_shapes=[pltpu.VMEM((tokens, model), F32)],
        compiler_params=params(),
        cost_estimate=cost(4 * tokens * features * model, 20 * tokens * features),
        name="middle",
    )(signal, gate_input, readout, log_decay, skip, gain, core, normed, out_weight, piece)
    layer_out = summed(layer_part, "head")
    later, parts, _ = entering(own_later, parts, True, fades)

    signal_grad, map_grad, read_grad, decay_grad = pl.pallas_call(
        backward_kernel,
        grid=(groups,),
        in_specs=[wide, wide, wide, narrow, narrow, logs, lane, entries, state],
        out_specs=[wide, narrow, narrow, logs],
        out_shape=[
            sds((tokens, features), F32),
            sds((tokens, groups * N), F32),
            sds((tokens, groups * N), F32),
            sds((heads, tokens), F32),
        ],
        compiler_params=params(),
        cost_estimate=cost(4 * tokens * features * model, 16 * tokens * features),
        name="backward",
    )(signal, dy, core, input_map, readout, log_decay, skip, entry, later)

    gain_grad = jnp.sum(parts[:, :, 0:3], axis=(0, 2)).reshape(features)
    skip_grad = jnp.sum(
        parts[:, :, 3:6].reshape(-1, groups, 3, in_group, P_SIZE), axis=(0, 2, 4)
    ).reshape(heads)
    return (
        layer_out,
        signal_grad,
        gate_grad,
        map_grad,
        read_grad,
        decay_grad,
        skip_grad,
        gain_grad,
        weight_grad,
    )


def solution(mesh):
    return jax.shard_map(
        on_device,
        mesh=mesh,
        in_specs=(
            P("ctx", "head"),
            P("ctx", "head"),
            P("ctx", "head"),
            P("ctx", "head"),
            P("head", "ctx"),
            P("head"),
            P("head"),
            P("head", None),
            P(("ctx", "head"), None),
        ),
        out_specs=(
            P(("ctx", "head"), None),
            P("ctx", "head"),
            P("ctx", "head"),
            P("ctx", "head"),
            P("ctx", "head"),
            P("head", "ctx"),
            P("head"),
            P("head"),
            P("head", None),
        ),
        check_vma=False,
    )
```

```python
from functools import partial

import jax
import jax.numpy as jnp
from jax import lax
from jax.experimental import pallas as pl
from jax.experimental.pallas import tpu as pltpu
from jax.sharding import PartitionSpec as P

P_SIZE = 64
N = 128
CHUNK = 256
F32 = jnp.float32
BF16 = jnp.bfloat16
VMEM_LIMIT = 52 * 1024 * 1024

NN = (((1,), (0,)), ((), ()))
NT = (((1,), (1,)), ((), ()))
TN = (((0,), (0,)), ((), ()))


def mm(a, b, dims=NN):
    return lax.dot_general(a, b, dims, preferred_element_type=F32)


def spread(factor, width):
    rows = factor.shape[0]
    left = lax.broadcasted_iota(jnp.int32, (rows, 128), 1) < P_SIZE
    pairs = []
    for k in range(width // 128):
        a = jnp.broadcast_to(factor[:, 2 * k : 2 * k + 1], (rows, 128))
        b = jnp.broadcast_to(factor[:, 2 * k + 1 : 2 * k + 2], (rows, 128))
        pairs.append(jnp.where(left, a, b))
    return jnp.concatenate(pairs, axis=1)


def cumulated(log_row):
    heads, length = log_row.shape
    hi = log_row.astype(BF16).astype(F32)
    rest = log_row - hi
    mid = rest.astype(BF16).astype(F32)
    low = rest - mid
    parts = jnp.concatenate([hi, mid, low, jnp.zeros_like(hi)], axis=0).astype(BF16)
    upper = (
        lax.broadcasted_iota(jnp.int32, (length, length), 0)
        <= lax.broadcasted_iota(jnp.int32, (length, length), 1)
    )
    sums = mm(parts, jnp.where(upper, 1.0, 0.0).astype(BF16))
    row = sums[0:heads] + sums[heads : 2 * heads] + sums[2 * heads : 3 * heads]
    col = jnp.transpose(jnp.concatenate([row] * (128 // heads), axis=0))
    return row, col


def decays(col, width):
    heads = width // P_SIZE
    col = col[:, :heads]
    from_start = jnp.exp(col)
    to_closing = jnp.exp(col[-1:, :] - col)
    return spread(from_start, width), spread(to_closing, width)


def chunks_of(total):
    return [(c, slice(c * CHUNK, (c + 1) * CHUNK)) for c in range(total // CHUNK)]


def in_parts(values):
    width = values[0].shape[1]
    at = lax.broadcasted_iota(jnp.int32, (8, width), 0)
    rows = jnp.zeros((8, width), F32)
    for i, value in enumerate(values):
        hi = value.astype(BF16).astype(F32)
        mid = (value - hi).astype(BF16).astype(F32)
        for j, part in enumerate((hi, mid, value - hi - mid)):
            rows = jnp.where(at == 3 * i + j, part, rows)
    return rows.astype(BF16)


def local_state_kernel(x_ref, b_ref, log_ref, state_ref, decay_ref):
    tokens, width = x_ref.shape
    state = jnp.zeros((N, width), F32)
    decay = jnp.ones((1, width), F32)
    for _, at in chunks_of(tokens):
        _, col = cumulated(log_ref[:, at])
        from_start, to_closing = decays(col, width)
        span = from_start[-1:, :]
        scaled = (x_ref[at, :].astype(F32) * to_closing).astype(BF16)
        state = state * span + mm(b_ref[at, :], scaled, TN)
        decay = decay * span
    state_ref[0] = state.astype(BF16)
    decay_ref[0] = in_parts([decay])


def forward_kernel(
    x_ref, z_ref, b_ref, c_ref, log_ref, skip_ref, gain_ref, incoming_ref, rows_ref,
    core_ref, entry_ref, normed_ref, weight_ref,
):
    tokens, width = x_ref.shape
    state = incoming_ref[0].astype(F32)
    left = lax.broadcasted_iota(jnp.int32, (CHUNK, 128), 1) < P_SIZE
    lower = (
        lax.broadcasted_iota(jnp.int32, (CHUNK, CHUNK), 0)
        >= lax.broadcasted_iota(jnp.int32, (CHUNK, CHUNK), 1)
    )
    last = tokens // CHUNK - 1
    for c, at in chunks_of(tokens):
        row, col = cumulated(log_ref[:, at])
        from_start, to_closing = decays(col, width)
        x = x_ref[at, :]
        xf = x.astype(F32)
        bm, cm = b_ref[at, :], c_ref[at, :]
        inner = mm(cm, bm, NT)
        entry = state.astype(BF16)
        entry_ref[0, c] = entry
        pieces = []
        for k in range(width // 128):
            pair = x[:, 128 * k : 128 * k + 128]
            halves = []
            for h in (2 * k, 2 * k + 1):
                gap = jnp.where(lower, col[:, h : h + 1] - row[h : h + 1, :], -1e30)
                halves.append(mm((jnp.exp(gap) * inner).astype(BF16), pair))
            pieces.append(jnp.where(left, halves[0], halves[1]))
        core = jnp.concatenate(pieces, axis=1) + from_start * mm(cm, entry)
        core_ref[at, :] = core
        y = core + skip_ref[...] * xf
        z = z_ref[at, :].astype(F32)
        gated = y * (z * jax.nn.sigmoid(z))
        inv = lax.rsqrt(jnp.mean(gated * gated, axis=1, keepdims=True) + 1e-05)
        normed_ref[at, :] = (gated * inv * gain_ref[...]).astype(BF16)
        if c < last:
            scaled = (xf * to_closing).astype(BF16)
            state = state * from_start[-1:, :] + mm(bm, scaled, TN)
    columns = rows_ref.shape[1]
    tile = 512
    for n in range(columns // tile):
        cut = slice(n * tile, (n + 1) * tile)
        weight_ref[:, cut] = mm(normed_ref[...], rows_ref[:, cut], TN).astype(BF16)


def middle_kernel(
    x_ref, z_ref, c_ref, log_ref, skip_ref, gain_ref, core_ref, normed_ref, w_ref, rows_ref,
    layer_ref, dy_ref, gate_ref, later_ref, part_ref, total,
):
    tokens, width = x_ref.shape
    group = pl.program_id(0)
    groups = pl.num_programs(0)
    outflow = jnp.zeros((N, width), F32)
    gain_sum = jnp.zeros((1, width), F32)
    skip_sum = jnp.zeros((1, width), F32)
    gain = gain_ref[...]
    for _, at in reversed(chunks_of(tokens)):
        _, col = cumulated(log_ref[:, at])
        from_start = spread(jnp.exp(col[:, : width // P_SIZE]), width)
        dn = mm(rows_ref[at, :], w_ref[...], NT).astype(BF16).astype(F32)
        xf = x_ref[at, :].astype(F32)
        z = z_ref[at, :].astype(F32)
        y = core_ref[at, :] + skip_ref[...] * xf
        s = jax.nn.sigmoid(z)
        silu = z * s
        gated = y * silu
        inv = lax.rsqrt(jnp.mean(gated * gated, axis=1, keepdims=True) + 1e-05)
        gain_sum += jnp.sum(dn * gated * inv, axis=0, keepdims=True)
        scaled = gain * dn
        mean = jnp.mean(scaled * gated, axis=1, keepdims=True)
        dgated = inv * scaled - gated * (inv * inv * inv * mean)
        gate_ref[at, :] = dgated * y * s * (1.0 + z * (1.0 - s))
        dy = dgated * silu
        dy_ref[at, :] = dy
        skip_sum += jnp.sum(dy * xf, axis=0, keepdims=True)
        outflow = outflow * from_start[-1:, :] + mm(
            c_ref[at, :], (dy * from_start).astype(BF16), TN
        )
    later_ref[0] = outflow.astype(BF16)
    part_ref[0] = in_parts([gain_sum, skip_sum])
    columns = w_ref.shape[1]
    tile = 512
    for n in range(columns // tile):
        cut = slice(n * tile, (n + 1) * tile)
        piece = mm(normed_ref[...], w_ref[:, cut])

        @pl.when(group == 0)
        def _():
            total[:, cut] = piece

        @pl.when(group > 0)
        def _():
            total[:, cut] += piece

    @pl.when(group == groups - 1)
    def _():
        layer_ref[...] = total[...].astype(BF16)


def backward_kernel(
    x_ref, dy_ref, core_ref, b_ref, c_ref, log_ref, skip_ref, entry_ref, later_ref,
    signal_ref, map_ref, read_ref, decay_ref,
):
    tokens, width = x_ref.shape
    heads = width // P_SIZE
    outflow = later_ref[0].astype(F32)
    left = lax.broadcasted_iota(jnp.int32, (CHUNK, 128), 1) < P_SIZE
    upper = (
        lax.broadcasted_iota(jnp.int32, (CHUNK, CHUNK), 0)
        <= lax.broadcasted_iota(jnp.int32, (CHUNK, CHUNK), 1)
    )
    own = (
        lax.broadcasted_iota(jnp.int32, (heads, width), 1) // P_SIZE
        == lax.broadcasted_iota(jnp.int32, (heads, width), 0)
    )
    own = jnp.where(own, 1.0, 0.0).astype(BF16)
    for c, at in reversed(chunks_of(tokens)):
        row, col = cumulated(log_ref[:, at])
        from_start, to_closing = decays(col, width)
        x = x_ref[at, :]
        xf = x.astype(F32)
        dyf = dy_ref[at, :]
        dy = dyf.astype(BF16)
        bm, cm = b_ref[at, :], c_ref[at, :]
        inner = mm(bm, cm, NT)
        out = outflow.astype(BF16)
        pair_sum = jnp.zeros((CHUNK, CHUNK), F32)
        pieces = []
        for k in range(width // 128):
            cut = slice(128 * k, 128 * k + 128)
            x_pair, dy_pair = x[:, cut], dy[:, cut]
            halves = []
            for h, side in ((2 * k, left), (2 * k + 1, ~left)):
                gap = jnp.where(upper, row[h : h + 1, :] - col[:, h : h + 1], -1e30)
                fade = jnp.exp(gap)
                halves.append(mm((fade * inner).astype(BF16), dy_pair))
                one = jnp.where(side, xf[:, cut], 0.0).astype(BF16)
                pair_sum += mm(one, dy_pair, NT) * fade
            pieces.append(jnp.where(left, halves[0], halves[1]))
        core_grad = jnp.concatenate(pieces, axis=1) + to_closing * mm(bm, out)
        signal_ref[at, :] = core_grad + skip_ref[...] * dyf
        pair_sum = pair_sum.astype(BF16)
        map_ref[at, :] = mm(pair_sum, cm) + mm((xf * to_closing).astype(BF16), out, NT)
        dy_start = (dyf * from_start).astype(BF16)
        read_ref[at, :] = mm(pair_sum, bm, TN) + mm(dy_start, entry_ref[0, c], NT)
        slope = dyf * core_ref[at, :] - xf * core_grad
        hi = slope.astype(BF16)
        low = (slope - hi.astype(F32)).astype(BF16)
        decay_ref[:, at] = mm(own, hi, NT) + mm(own, low, NT)
        if c > 0:
            outflow = outflow * from_start[-1:, :] + mm(cm, dy_start, TN)


def params():
    return pltpu.CompilerParams(
        dimension_semantics=("arbitrary",), vmem_limit_bytes=VMEM_LIMIT
    )


def cost(flops, moved, exps=0):
    return pl.CostEstimate(flops=int(flops), bytes_accessed=int(moved), transcendentals=int(exps))


def entering(state, extra, reverse, fades=None):
    devices = lax.axis_size("ctx")
    groups, depth, width = state.shape
    share = depth // devices
    shares = state.reshape(groups, devices, share, width).transpose(1, 0, 2, 3)
    copies = jnp.broadcast_to(extra[None], (devices,) + extra.shape)
    sent = jnp.concatenate([shares, copies], axis=2)
    every = lax.all_to_all(sent, "ctx", split_axis=0, concat_axis=0, tiled=True)
    extras = every[:, :, share:].astype(F32)
    if fades is None:
        fades = jnp.sum(extras[:, :, 0:3], axis=2, keepdims=True)
    carried = jnp.zeros((groups, share, width), F32)
    found = [None] * devices
    for d in reversed(range(devices)) if reverse else range(devices):
        found[d] = carried.astype(BF16)
        carried = fades[d] * carried + every[d, :, :share].astype(F32)
    back = lax.all_to_all(jnp.stack(found), "ctx", split_axis=0, concat_axis=0, tiled=True)
    return back.transpose(1, 0, 2, 3).reshape(groups, depth, width), extras, fades


def summed(part, axis):
    devices = lax.axis_size(axis)
    rows, columns = part.shape
    terms = lax.all_to_all(part, axis, split_axis=0, concat_axis=0, tiled=True)
    terms = terms.reshape(devices, rows // devices, columns)
    return jnp.sum(terms.astype(F32), axis=0).astype(BF16)


def on_device(
    signal, gate_input, input_map, readout, log_decay, skip_gain, norm_gain, out_weight, out_grad
):
    tokens, features = signal.shape
    heads = log_decay.shape[0]
    groups = input_map.shape[1] // N
    in_group = heads // groups
    width = in_group * P_SIZE
    model = out_weight.shape[1]
    spans = tokens // CHUNK
    sds = jax.ShapeDtypeStruct
    wide = pl.BlockSpec((tokens, width), lambda g: (0, g))
    narrow = pl.BlockSpec((tokens, N), lambda g: (0, g))
    logs = pl.BlockSpec((in_group, tokens), lambda g: (g, 0))
    lane = pl.BlockSpec((1, width), lambda g: (0, g))
    state = pl.BlockSpec((1, N, width), lambda g: (g, 0, 0))
    fade = pl.BlockSpec((1, 8, width), lambda g: (g, 0, 0))
    entries = pl.BlockSpec((1, spans, N, width), lambda g: (g, 0, 0, 0))
    weight = pl.BlockSpec((width, model), lambda g: (g, 0))
    rows = pl.BlockSpec((tokens, model), lambda g: (0, 0))

    skip = jnp.repeat(skip_gain, P_SIZE).reshape(1, features)
    gain = norm_gain.reshape(1, features)
    piece = lax.all_gather(out_grad, "head", axis=0, tiled=True)

    own_state, own_fade = pl.pallas_call(
        local_state_kernel,
        grid=(groups,),
        in_specs=[wide, narrow, logs],
        out_specs=[state, fade],
        out_shape=[sds((groups, N, width), BF16), sds((groups, 8, width), BF16)],
        compiler_params=params(),
        cost_estimate=cost(2 * tokens * N * features, 3 * tokens * features),
        name="local_state",
    )(signal, input_map, log_decay)
    incoming, _, fades = entering(own_state, own_fade, False)

    core, entry, normed, weight_part = pl.pallas_call(
        forward_kernel,
        grid=(groups,),
        in_specs=[wide, wide, narrow, narrow, logs, lane, lane, state, rows],
        out_specs=[wide, entries, wide, weight],
        out_shape=[
            sds((tokens, features), F32),
            sds((groups, spans, N, width), BF16),
            sds((tokens, features), BF16),
            sds((features, model), BF16),
        ],
        compiler_params=params(),
        cost_estimate=cost(2 * tokens * features * model, 12 * tokens * features),
        name="forward",
    )(signal, gate_input, input_map, readout, log_decay, skip, gain, incoming, piece)
    half = features // 2
    weight_halves = []
    for at in (slice(0, half), slice(half, features)):
        weight_share = summed(weight_part[at], "ctx")
        weight_halves.append(lax.all_gather(weight_share, "ctx", axis=0, tiled=True))
    weight_grad = jnp.concatenate([part.astype(F32) for part in weight_halves], axis=0)

    layer_part, dy, gate_grad, own_later, parts = pl.pallas_call(
        middle_kernel,
        grid=(groups,),
        in_specs=[wide, wide, narrow, logs, lane, lane, wide, wide, weight, rows],
        out_specs=[rows, wide, wide, state, fade],
        out_shape=[
            sds((tokens, model), BF16),
            sds((tokens, features), F32),
            sds((tokens, features), F32),
            sds((groups, N, width), BF16),
            sds((groups, 8, width), BF16),
        ],
        scratch_shapes=[pltpu.VMEM((tokens, model), F32)],
        compiler_params=params(),
        cost_estimate=cost(4 * tokens * features * model, 20 * tokens * features),
        name="middle",
    )(signal, gate_input, readout, log_decay, skip, gain, core, normed, out_weight, piece)
    layer_out = summed(layer_part, "head")
    later, parts, _ = entering(own_later, parts, True, fades)

    signal_grad, map_grad, read_grad, decay_grad = pl.pallas_call(
        backward_kernel,
        grid=(groups,),
        in_specs=[wide, wide, wide, narrow, narrow, logs, lane, entries, state],
        out_specs=[wide, narrow, narrow, logs],
        out_shape=[
            sds((tokens, features), F32),
            sds((tokens, groups * N), F32),
            sds((tokens, groups * N), F32),
            sds((heads, tokens), F32),
        ],
        compiler_params=params(),
        cost_estimate=cost(4 * tokens * features * model, 16 * tokens * features),
        name="backward",
    )(signal, dy, core, input_map, readout, log_decay, skip, entry, later)

    gain_grad = jnp.sum(parts[:, :, 0:3], axis=(0, 2)).reshape(features)
    skip_grad = jnp.sum(
        parts[:, :, 3:6].reshape(-1, groups, 3, in_group, P_SIZE), axis=(0, 2, 4)
    ).reshape(heads)
    return (
        layer_out,
        signal_grad,
        gate_grad,
        map_grad,
        read_grad,
        decay_grad,
        skip_grad,
        gain_grad,
        weight_grad,
    )


def solution(mesh):
    return jax.shard_map(
        on_device,
        mesh=mesh,
        in_specs=(
            P("ctx", "head"),
            P("ctx", "head"),
            P("ctx", "head"),
            P("ctx", "head"),
            P("head", "ctx"),
            P("head"),
            P("head"),
            P("head", None),
            P(("ctx", "head"), None),
        ),
        out_specs=(
            P(("ctx", "head"), None),
            P("ctx", "head"),
            P("ctx", "head"),
            P("ctx", "head"),
            P("ctx", "head"),
            P("head", "ctx"),
            P("head"),
            P("head"),
            P("head", None),
        ),
        check_vma=False,
    )
```
